32 devices in a mesh: shot: 8 (over z, x), space: 4 (over y, core).
Axes of the slice: x: 2, y: 2, z: 4, core: 2. Of those that a mesh axis runs over, the one named last changes fastest.
Arguments:
- wavefields: float32 [8, 2, 4, 64, 128, 128], P('shot', None, None, 'space'), may hold values from -6 to 6
- velocity_sq: float32 [64, 256, 128], P('space', 'shot'), may hold values from 0.04 to 0.12
- epsilon: float32 [64, 256, 128], P('space', 'shot'), may hold values from 0 to 0.3
- delta: float32 [64, 256, 128], P('space', 'shot'), may hold values from -0.05 to 0.2
- trace_rows: float32 [2048, 128], P(('shot', 'space')), may hold values from -6 to 6
- receiver_rows: int32 [8, 64, 32], replicated, may hold values from 0 to 2047, as said below
- anchors: int32 [8], replicated, may hold values from 0 to 128, as said below
Outputs:
- new_fields: float32 [8, 4, 64, 128, 128], P('shot', None, 'space')
- gradient: float32 [64, 256, 128], P('space', 'shot')
The draws below stay inside these ranges and needn't reach their ends.
Inputs may be any that keep to these rules, and one draw needn't show every extreme that they name: Row r is stored on the device of index r // 64 along shot+space (shot first). Device (s, p) reads the rows receiver_rows[s, p*16 to (p+1)*16 - 1, :]; among these 512 entries at most 32 name rows of any one storing device, and exactly 32 do for some storing device. anchors[s] lies between 32 * (s - 3) and 32 * s.
All inputs are finite; a program needn't handle non-finite values.
Results may differ from the reference program's by a relative error of at most 0.0003.
Values sent between devices are 32-bit elements; how exact they have to be, the bound alone decides.
No kernel may reach another device: no remote copies, remote signals or barrier semaphores. Data moves between devices by JAX's collectives and lax.ppermute only.
A program may use at most 128 MiB of HBM per device.

```python
import math
import jax
import jax.numpy as jnp
from jax import lax

CX = 16
CY = 128
NZ = 128
RDEP = 32
ROWS_DEV = 64
SHOTS = 8
NX = 64
G = 32
GY = 256
ROWS = 2048
CAP = 32


def draw_receiver_rows(key, part):
    blocks = SHOTS * NX // CX
    devices = ROWS // ROWS_DEV
    asked_rows = CX * RDEP
    first_key, second_key, third_key = jax.random.split(key, 3)
    orders = jax.vmap(lambda one_key: jax.random.permutation(one_key, devices))(jax.random.split(first_key, blocks))
    least = (asked_rows - CAP + devices - 2) // (devices - 1)
    group = jax.random.randint(second_key, (blocks, 1), least, CAP + 1)
    position = jnp.arange(asked_rows, dtype=jnp.int32)[None, :]
    which = jnp.where(position < CAP, 0, 1 + (position - CAP) // group)
    owners = jnp.take_along_axis(orders, which, axis=1)
    local_rows = jax.random.randint(third_key, (blocks, asked_rows), 0, ROWS_DEV)
    return (owners * ROWS_DEV + local_rows).astype(jnp.int32).reshape(SHOTS, NX, RDEP)


def draw_anchors(key, part):
    shot_numbers = jnp.arange(SHOTS, dtype=jnp.int32)
    jitter = jax.random.randint(key, (SHOTS,), 0, 3 * G + 1)
    return jnp.clip(shot_numbers * G - 3 * G + jitter, 0, GY - CY).astype(jnp.int32)


def level_of(own_key, extent, pieces, smallest, top_value):
    loudness = 1.0
    for dim, shards_of in pieces:
        steps = jax.random.uniform(jax.random.fold_in(jax.random.fold_in(own_key, 6), dim), (shards_of,), jnp.float32, smallest / len(pieces), top_value / len(pieces))
        loudness = loudness * jnp.repeat(jnp.exp(steps), extent[dim] // shards_of).reshape((-1,) + (1,) * (len(extent) - 1 - dim))
    return loudness


def centred(key, dims, spread, reach, pieces=(), held_as=jnp.bfloat16):
    factor_of = level_of(key, dims, pieces, -0.22, 0.18) if pieces else 1.0
    drawn = jax.random.normal(key, dims, jnp.float32) * spread * factor_of
    return jnp.minimum(jnp.maximum(drawn, -reach), reach).astype(held_as)


def setup_inputs(seed: int = 0) -> dict:
    seeds = jax.random.split(jax.random.key(seed), 8)
    return {
        "wavefields": centred(seeds[0], (SHOTS, 2, 4, NX, CY, NZ), 1.0, 6.0, ((0, 8), (3, 4)), jnp.float32),
        "velocity_sq": jnp.clip(jnp.exp(math.log(0.12) - 1.0986123 * jax.random.uniform(seeds[1], (NX, GY, NZ), jnp.float32) ** level_of(seeds[1], (NX, GY, NZ), ((0, 4), (1, 8)), -0.2, 0.2)), 0.04, 0.12),
        "epsilon": jnp.clip(0.3 * jax.random.uniform(seeds[2], (NX, GY, NZ), jnp.float32) ** level_of(seeds[2], (NX, GY, NZ), ((0, 4), (1, 8)), -0.2, 0.2), 0.0, 0.3),
        "delta": jnp.clip(-0.05 + 0.25 * jax.random.uniform(seeds[3], (NX, GY, NZ), jnp.float32) ** level_of(seeds[3], (NX, GY, NZ), ((0, 4), (1, 8)), -0.2, 0.2), -0.05, 0.2),
        "trace_rows": centred(seeds[4], (ROWS, CY), 1.0, 6.0, ((0, 32),), jnp.float32),
        "receiver_rows": draw_receiver_rows(jax.random.fold_in(seeds[7], 71), 0),
        "anchors": draw_anchors(jax.random.fold_in(seeds[7], 71), 0),
    }


coefficients = (-205.0 / 72.0, 8.0 / 5.0, -1.0 / 5.0, 8.0 / 315.0, -1.0 / 560.0)
image_scale = 0.1

def from_padded(padded, axis_number, length):
    summed = coefficients[0] * lax.slice_in_dim(padded, 4, 4 + length, axis=axis_number)
    for offset in range(1, 5):
        summed = summed + coefficients[offset] * (lax.slice_in_dim(padded, 4 + offset, 4 + offset + length, axis=axis_number) + lax.slice_in_dim(padded, 4 - offset, 4 - offset + length, axis=axis_number))
    return summed

def second_derivative(values, axis_number):
    widths = [(4, 4) if dimension == axis_number else (0, 0) for dimension in range(values.ndim)]
    return from_padded(jnp.pad(values, widths), axis_number, values.shape[axis_number])

def place_sources(rows_in, depth_cells):
    spacing = depth_cells // rows_in.shape[1]
    before = spacing // 2
    turned = jnp.transpose(rows_in, (0, 2, 1))[..., None]
    padded = jnp.pad(turned, ((0, 0), (0, 0), (0, 0), (before, spacing - before - 1)))
    return padded.reshape(turned.shape[0], turned.shape[1], depth_cells)

def propagate(previous, current, padded_main, velocity, stretch, coupling, sources):
    cells_x = current.shape[1]
    horizontal = from_padded(padded_main, 1, cells_x) + second_derivative(current[0:2], 2)
    vertical = second_derivative(current[2:4], 3)
    main_forward = stretch * horizontal[0] + coupling * vertical[0]
    second_forward = coupling * horizontal[0] + vertical[0]
    main_adjoint = stretch * horizontal[1] + coupling * vertical[1]
    second_adjoint = coupling * horizontal[1] + vertical[1]
    fields = jnp.stack([2.0 * current[0] - previous[0] + velocity * main_forward, 2.0 * current[1] - previous[1] + velocity * (main_adjoint + sources), 2.0 * current[2] - previous[2] + velocity * second_forward, 2.0 * current[3] - previous[3] + velocity * second_adjoint])
    image = image_scale * (fields[1] * main_forward + fields[3] * second_forward)
    return (fields, image)

def reference(wavefields, velocity_sq, epsilon, delta, trace_rows, receiver_rows, anchors):

    def one_shot(gradient, inputs):
        fields, requests, anchor = inputs
        zero_index = jnp.zeros((), jnp.int32)
        corner = (zero_index, anchor.astype(jnp.int32), zero_index)
        velocity = lax.dynamic_slice(velocity_sq, corner, (NX, CY, NZ))
        stretch = 1.0 + 2.0 * lax.dynamic_slice(epsilon, corner, (NX, CY, NZ))
        coupling = jnp.sqrt(1.0 + 2.0 * lax.dynamic_slice(delta, corner, (NX, CY, NZ)))
        sources = place_sources(trace_rows[requests], NZ)
        current = fields[1]
        padded_main = jnp.pad(current[0:2], ((0, 0), (4, 4), (0, 0), (0, 0)))
        next_fields, image = propagate(fields[0], current, padded_main, velocity, stretch, coupling, sources)
        window = lax.dynamic_slice(gradient, corner, (NX, CY, NZ))
        gradient = lax.dynamic_update_slice(gradient, window + image, corner)
        return (gradient, next_fields)
    gradient, new_fields = lax.scan(one_shot, jnp.zeros((NX, GY, NZ), jnp.float32), (wavefields, receiver_rows, anchors))
    return (new_fields, gradient)
```

```python
import jax
import jax.numpy as jnp
from jax import lax
from jax.sharding import PartitionSpec as P

coefficients = (-205.0 / 72.0, 8.0 / 5.0, -1.0 / 5.0, 8.0 / 315.0, -1.0 / 560.0)
image_scale = 0.1
reach = 3


def shift(values, axis, by):
    count = lax.axis_size(axis)
    pairs = [(i, i + by) for i in range(count) if 0 <= i + by < count]
    return lax.ppermute(values, axis, pairs)


def cycle(values, axis, by):
    count = lax.axis_size(axis)
    return lax.ppermute(values, axis, [(i, (i + by) % count) for i in range(count)])


def swap(values, axis):
    return lax.ppermute(values, axis, [(i, i ^ 1) for i in range(lax.axis_size(axis))])


def outward(values, axis):
    count = lax.axis_size(axis)
    pairs = [(i, i + 1 if i % 2 else i - 1) for i in range(count)]
    return lax.ppermute(values, axis, [(i, j) for i, j in pairs if 0 <= j < count])


def from_padded(padded, axis_number, length):
    summed = coefficients[0] * lax.slice_in_dim(padded, 4, 4 + length, axis=axis_number)
    for offset in range(1, 5):
        summed = summed + coefficients[offset] * (
            lax.slice_in_dim(padded, 4 + offset, 4 + offset + length, axis=axis_number)
            + lax.slice_in_dim(padded, 4 - offset, 4 - offset + length, axis=axis_number)
        )
    return summed


def second_derivative(values, axis_number):
    widths = [(4, 4) if dimension == axis_number else (0, 0) for dimension in range(values.ndim)]
    return from_padded(jnp.pad(values, widths), axis_number, values.shape[axis_number])


def place_sources(rows_in, depth_cells):
    levels = rows_in.shape[1]
    spacing = depth_cells // levels
    targets = jnp.arange(levels, dtype=jnp.int32) * spacing + spacing // 2
    depth_ids = jnp.arange(depth_cells, dtype=jnp.int32)
    onehot = (targets[:, None] == depth_ids[None, :]).astype(jnp.float32)
    return jnp.einsum("xjy,jz->xyz", rows_in, onehot, precision=lax.Precision.HIGHEST)


def gather_traces(rows):
    parts = [rows] + [cycle(rows, "shot", k) for k in range(2, lax.axis_size("shot"), 2)]
    rows = jnp.concatenate(parts)
    rows = jnp.concatenate([rows, swap(rows, "shot")])
    parts = [rows] + [cycle(rows, "space", k) for k in range(2, lax.axis_size("space"), 2)]
    rows = jnp.concatenate(parts)
    return jnp.concatenate([rows, swap(rows, "space")])


def row_positions(requests, rows_each, shot, space):
    half_shots = lax.axis_size("shot") // 2
    half_spaces = lax.axis_size("space") // 2
    owner = requests // rows_each
    of_shot = owner // (2 * half_spaces)
    of_space = owner % (2 * half_spaces)
    core = (of_space + space) % 2
    down_y = (space // 2 - of_space // 2) % half_spaces
    across = (of_shot + shot) % 2
    down_z = (shot // 2 - of_shot // 2) % half_shots
    block = ((core * half_spaces + down_y) * 2 + across) * half_shots + down_z
    return block * rows_each + requests % rows_each


def local(wavefields, velocity_sq, epsilon, delta, trace_rows, receiver_rows, anchors):
    shot = lax.axis_index("shot")
    space = lax.axis_index("space")
    shot_count = lax.axis_size("shot")
    odd = shot % 2 == 1
    cells_x, cells_y, cells_z = wavefields.shape[3:]
    width = velocity_sq.shape[1]
    levels = receiver_rows.shape[2]
    anchor = lax.dynamic_index_in_dim(anchors, shot, 0, keepdims=False)
    partner_anchor = lax.dynamic_index_in_dim(anchors, shot + 1 - 2 * (shot % 2), 0, keepdims=False)
    lower_columns = (shot - 2) * width + jnp.arange(width, dtype=jnp.int32)
    from_lower = (lower_columns >= partner_anchor)[None, :, None]

    own = jnp.stack([velocity_sq, epsilon, delta])
    below = shift(own, "shot", 2)
    above = shift(own, "shot", -2)
    beside = swap(own, "shot")

    previous = wavefields[0, 0]
    current = wavefields[0, 1]
    main = current[0:2]
    before = shift(main[:, cells_x - 4 :], "space", 1)
    after = shift(main[:, :4], "space", -1)
    everything = gather_traces(trace_rows)
    requests = lax.dynamic_slice(
        receiver_rows, (shot, space * cells_x, jnp.zeros((), jnp.int32)), (1, cells_x, levels)
    )
    positions = row_positions(requests.reshape(-1), trace_rows.shape[0], shot, space)
    rows_in = everything[positions].reshape(cells_x, levels, cells_y)
    sources = place_sources(rows_in, cells_z)

    merged = swap(jnp.where(from_lower[None], below, above), "shot")
    far = outward(jnp.where(odd, below, above), "shot")
    joined = jnp.concatenate(
        [
            jnp.where(odd, merged, far),
            below,
            jnp.where(odd, beside, merged),
            own,
            jnp.where(odd, merged, beside),
            above,
            jnp.where(odd, far, merged),
        ],
        axis=2,
    )
    zero = jnp.zeros((), jnp.int32)
    start = anchor - (shot - reach) * width
    window = lax.dynamic_slice(joined, (zero, zero, start, zero), (3, cells_x, cells_y, cells_z))
    velocity = window[0]
    stretch = 1.0 + 2.0 * window[1]
    coupling = jnp.sqrt(1.0 + 2.0 * window[2])

    padded_main = jnp.concatenate([before, main, after], axis=1)
    horizontal = from_padded(padded_main, 1, cells_x) + second_derivative(main, 2)
    vertical = second_derivative(current[2:4], 3)
    main_forward = stretch * horizontal[0] + coupling * vertical[0]
    second_forward = coupling * horizontal[0] + vertical[0]
    main_adjoint = stretch * horizontal[1] + coupling * vertical[1]
    second_adjoint = coupling * horizontal[1] + vertical[1]
    fields = jnp.stack(
        [
            2.0 * current[0] - previous[0] + velocity * main_forward,
            2.0 * current[1] - previous[1] + velocity * (main_adjoint + sources),
            2.0 * current[2] - previous[2] + velocity * second_forward,
            2.0 * current[3] - previous[3] + velocity * second_adjoint,
        ]
    )
    image = image_scale * (fields[1] * main_forward + fields[3] * second_forward)

    wide = jnp.zeros((cells_x, (2 * reach + 1) * width, cells_z), jnp.float32)
    wide = lax.dynamic_update_slice(wide, image, (zero, start, zero))
    piece = {
        k: wide[:, (k + reach) * width : (k + reach + 1) * width] for k in range(-reach, reach + 1)
    }
    merged = swap(jnp.where(odd, piece[-3] + piece[1], piece[-1] + piece[3]), "shot")
    far = outward(jnp.where(odd, piece[3], piece[-3]), "shot")
    beside = swap(jnp.where(odd, piece[-1], piece[1]), "shot")
    nothing = jnp.zeros((), jnp.float32)
    down = piece[-2] + jnp.where(from_lower, merged, nothing) + jnp.where(odd, far, nothing)
    up = piece[2] + jnp.where(from_lower, nothing, merged) + jnp.where(odd, nothing, far)
    gradient = piece[0] + beside + shift(down, "shot", -2) + shift(up, "shot", 2)
    return (fields[None], gradient)


def solution(mesh):
    in_specs = (
        P("shot", None, None, "space", None, None),
        P("space", "shot", None),
        P("space", "shot", None),
        P("space", "shot", None),
        P(("shot", "space"), None),
        P(),
        P(),
    )
    out_specs = (P("shot", None, "space", None, None), P("space", "shot", None))
    return jax.shard_map(local, mesh=mesh, in_specs=in_specs, out_specs=out_specs, check_vma=False)
```

```python
import functools

import jax
import jax.numpy as jnp
from jax import lax
from jax.experimental import pallas as pl
from jax.experimental.pallas import tpu as pltpu
from jax.sharding import PartitionSpec as P

coefficients = (-205.0 / 72.0, 8.0 / 5.0, -1.0 / 5.0, 8.0 / 315.0, -1.0 / 560.0)
image_scale = 0.1
reach = 3


def shift(values, axis, by):
    count = lax.axis_size(axis)
    pairs = [(i, i + by) for i in range(count) if 0 <= i + by < count]
    return lax.ppermute(values, axis, pairs)


def cycle(values, axis, by):
    count = lax.axis_size(axis)
    return lax.ppermute(values, axis, [(i, (i + by) % count) for i in range(count)])


def swap(values, axis):
    return lax.ppermute(values, axis, [(i, i ^ 1) for i in range(lax.axis_size(axis))])


def parted(values, axis, by):
    count = lax.axis_size(axis)
    pairs = [(i, i + by if i % 2 else i - by) for i in range(count)]
    return lax.ppermute(values, axis, [(i, j) for i, j in pairs if 0 <= j < count])


def banded(cells):
    rows = lax.broadcasted_iota(jnp.int32, (cells, cells), 0)
    columns = lax.broadcasted_iota(jnp.int32, (cells, cells), 1)
    distance = jnp.abs(rows - columns)
    band = jnp.zeros((cells, cells), jnp.float32)
    for k, coefficient in enumerate(coefficients):
        band = jnp.where(distance == k, jnp.float32(coefficient), band)
    return band


def times(left, right):
    return lax.dot_general(
        left,
        right,
        (((1,), (0,)), ((), ())),
        precision=lax.Precision.HIGHEST,
        preferred_element_type=jnp.float32,
    )


def derive_kernel(layers, wave, before, after, previous, second, across, along, base, padded, sems):
    cells_x = wave.shape[3]
    step = pl.program_id(0)

    @pl.when(step == 0)
    def _():
        copies = [
            pltpu.make_async_copy(before, padded.at[:, pl.ds(0, 4)], sems.at[0]),
            pltpu.make_async_copy(
                wave.at[0, 1, pl.ds(0, 2)], padded.at[:, pl.ds(4, cells_x)], sems.at[1]
            ),
            pltpu.make_async_copy(after, padded.at[:, pl.ds(4 + cells_x, 4)], sems.at[2]),
        ]
        for copy in copies:
            copy.start()
        for copy in copies:
            copy.wait()

    band_y = banded(padded.shape[2])
    band_z = band_y if padded.shape[2] == padded.shape[3] else banded(padded.shape[3])
    for layer in range(layers):
        at = step * layers + layer + 4
        for f in range(2):
            centre = padded[f, at]
            total = coefficients[0] * centre
            for k in range(1, 5):
                total = total + coefficients[k] * (padded[f, at + k] + padded[f, at - k])
            across[f, layer] = total + times(band_y, centre)
            base[f, layer] = 2.0 * centre - previous[0, 0, f, layer]
        for f in range(2):
            values = second[0, 0, f, layer]
            along[f, layer] = times(values, band_z)
            base[2 + f, layer] = 2.0 * values - previous[0, 0, 2 + f, layer]


def derive(wavefields, before, after):
    cells_x, cells_y, cells_z = wavefields.shape[3:]
    layers = 2

    def field(count):
        return (count, layers, cells_y, cells_z)

    out = [
        jax.ShapeDtypeStruct((count, cells_x, cells_y, cells_z), jnp.float32) for count in (2, 2, 4)
    ]
    return pl.pallas_call(
        functools.partial(derive_kernel, layers),
        grid=(cells_x // layers,),
        in_specs=[
            pl.BlockSpec(memory_space=pl.ANY),
            pl.BlockSpec(memory_space=pl.ANY),
            pl.BlockSpec(memory_space=pl.ANY),
            pl.BlockSpec((1, 1) + field(4), lambda i: (0, 0, 0, i, 0, 0)),
            pl.BlockSpec((1, 1) + field(2), lambda i: (0, 1, 1, i, 0, 0)),
        ],
        out_specs=[pl.BlockSpec(field(count), lambda i: (0, i, 0, 0)) for count in (2, 2, 4)],
        out_shape=out,
        scratch_shapes=[
            pltpu.VMEM((2, cells_x + 8, cells_y, cells_z), jnp.float32),
            pltpu.SemaphoreType.DMA((3,)),
        ],
        compiler_params=pltpu.CompilerParams(vmem_limit_bytes=16 << 20),
        cost_estimate=pl.CostEstimate(
            flops=40 * wavefields.size, bytes_accessed=8 * wavefields.size, transcendentals=0
        ),
        name="derive",
    )(wavefields, before, after, wavefields, wavefields)


def finish_kernel(layers, scalars, *refs):
    velocity, epsilon, delta, far, inner, outer, beside, merged = refs[:8]
    across, along, base, rows = refs[8:12]
    fields, own_image, far_image, inner_image, outer_image, beside_image, merged_image = refs[12:19]
    joined, wide = refs[19:]
    width = own_image.shape[1]
    cells_y, cells_z = base.shape[2:]
    start = scalars[0]
    odd = scalars[1]

    def slot(when_odd, when_even):
        return pl.ds(pl.multiple_of(jnp.where(odd == 1, when_odd, when_even) * width, width), width)

    far_slot, inner_slot, outer_slot = slot(6, 0), slot(1, 5), slot(5, 1)
    beside_slot, merged_slots = slot(2, 4), (slot(0, 2), slot(4, 6))
    own_slot = pl.ds(3 * width, width)

    @pl.when(pl.program_id(0) == 0)
    def _():
        wide[...] = jnp.zeros_like(wide)

    levels = rows.shape[1]
    spacing = cells_z // levels
    level = lax.broadcasted_iota(jnp.int32, (levels, cells_z), 0)
    depth = lax.broadcasted_iota(jnp.int32, (levels, cells_z), 1)
    placing = jnp.where(depth == level * spacing + spacing // 2, 1.0, 0.0).astype(jnp.float32)
    for layer in range(layers):
        for k, own in enumerate((velocity, epsilon, delta)):
            joined[k, own_slot] = own[layer]
            joined[k, far_slot] = far[k, layer]
            joined[k, inner_slot] = inner[k, layer]
            joined[k, outer_slot] = outer[k, layer]
            joined[k, beside_slot] = beside[k, layer]
            for one in merged_slots:
                joined[k, one] = merged[k, layer]
        window = pl.ds(start, cells_y)
        speed = joined[0, window]
        stretch = 1.0 + 2.0 * joined[1, window]
        coupling = jnp.sqrt(1.0 + 2.0 * joined[2, window])
        sources = lax.dot_general(
            rows[layer],
            placing,
            (((0,), (0,)), ((), ())),
            precision=lax.Precision.HIGHEST,
            preferred_element_type=jnp.float32,
        )
        main_forward = stretch * across[0, layer] + coupling * along[0, layer]
        second_forward = coupling * across[0, layer] + along[0, layer]
        main_adjoint = stretch * across[1, layer] + coupling * along[1, layer]
        second_adjoint = coupling * across[1, layer] + along[1, layer]
        new_adjoint = base[1, layer] + speed * (main_adjoint + sources)
        new_second = base[3, layer] + speed * second_adjoint
        fields[0, 0, layer] = base[0, layer] + speed * main_forward
        fields[0, 1, layer] = new_adjoint
        fields[0, 2, layer] = base[2, layer] + speed * second_forward
        fields[0, 3, layer] = new_second
        wide[window] = image_scale * (new_adjoint * main_forward + new_second * second_forward)
        own_image[layer] = wide[own_slot]
        far_image[layer] = wide[far_slot]
        inner_image[layer] = wide[inner_slot]
        outer_image[layer] = wide[outer_slot]
        beside_image[layer] = wide[beside_slot]
        merged_image[layer] = wide[merged_slots[0]] + wide[merged_slots[1]]


def finish(scalars, model, pieces, across, along, base, rows):
    cells_x, width, cells_z = model[0].shape
    cells_y = base.shape[2]
    layers = 2
    slab = pl.BlockSpec((layers, width, cells_z), lambda i, _: (i, 0, 0))
    stacked = pl.BlockSpec((3, layers, width, cells_z), lambda i, _: (0, i, 0, 0))

    def field(count):
        return pl.BlockSpec((count, layers, cells_y, cells_z), lambda i, _: (0, i, 0, 0))

    return pl.pallas_call(
        functools.partial(finish_kernel, layers),
        grid_spec=pltpu.PrefetchScalarGridSpec(
            num_scalar_prefetch=1,
            grid=(cells_x // layers,),
            in_specs=[slab] * 3
            + [stacked] * 5
            + [field(2), field(2), field(4)]
            + [pl.BlockSpec((layers,) + rows.shape[1:], lambda i, _: (i, 0, 0))],
            out_specs=[
                pl.BlockSpec((1, 4, layers, cells_y, cells_z), lambda i, _: (0, 0, i, 0, 0))
            ]
            + [slab] * 6,
            scratch_shapes=[
                pltpu.VMEM((3, (2 * reach + 1) * width, cells_z), jnp.float32),
                pltpu.VMEM(((2 * reach + 1) * width, cells_z), jnp.float32),
            ],
        ),
        out_shape=[jax.ShapeDtypeStruct((1,) + base.shape, jnp.float32)]
        + [jax.ShapeDtypeStruct(model[0].shape, jnp.float32)] * 6,
        compiler_params=pltpu.CompilerParams(vmem_limit_bytes=16 << 20),
        cost_estimate=pl.CostEstimate(
            flops=10 * base.size, bytes_accessed=16 * base.size, transcendentals=0
        ),
        name="finish",
    )(scalars, *model, *pieces, across, along, base, rows)


def gather_traces(rows):
    parts = [rows] + [cycle(rows, "shot", k) for k in range(2, lax.axis_size("shot"), 2)]
    rows = jnp.concatenate(parts)
    rows = jnp.concatenate([rows, swap(rows, "shot")])
    parts = [rows] + [cycle(rows, "space", k) for k in range(2, lax.axis_size("space"), 2)]
    rows = jnp.concatenate(parts)
    return jnp.concatenate([rows, swap(rows, "space")])


def row_positions(requests, rows_each, shot, space):
    half_shots = lax.axis_size("shot") // 2
    half_spaces = lax.axis_size("space") // 2
    owner = requests // rows_each
    of_shot = owner // (2 * half_spaces)
    of_space = owner % (2 * half_spaces)
    core = (of_space + space) % 2
    down_y = (space // 2 - of_space // 2) % half_spaces
    across = (of_shot + shot) % 2
    down_z = (shot // 2 - of_shot // 2) % half_shots
    block = ((core * half_spaces + down_y) * 2 + across) * half_shots + down_z
    return block * rows_each + requests % rows_each


def local(wavefields, velocity_sq, epsilon, delta, trace_rows, receiver_rows, anchors):
    shot = lax.axis_index("shot")
    space = lax.axis_index("space")
    odd = shot % 2 == 1
    cells_x, cells_y, cells_z = wavefields.shape[3:]
    width = velocity_sq.shape[1]
    levels = receiver_rows.shape[2]
    anchor = lax.dynamic_index_in_dim(anchors, shot, 0, keepdims=False)
    partner_anchor = lax.dynamic_index_in_dim(anchors, shot + 1 - 2 * (shot % 2), 0, keepdims=False)
    lower_columns = (shot - 2) * width + jnp.arange(width, dtype=jnp.int32)
    from_lower = (lower_columns >= partner_anchor)[None, :, None]
    from_inner = from_lower == odd

    own = jnp.stack([velocity_sq, epsilon, delta])
    inner = parted(own, "shot", 2)
    outer = parted(own, "shot", -2)
    beside = swap(own, "shot")

    main = wavefields[0, 1, 0:2]
    before = shift(main[:, cells_x - 4 :], "space", 1)
    after = shift(main[:, :4], "space", -1)
    across, along, base = derive(wavefields, before, after)

    everything = gather_traces(trace_rows)
    requests = lax.dynamic_slice(
        receiver_rows, (shot, space * cells_x, jnp.zeros((), jnp.int32)), (1, cells_x, levels)
    )
    positions = row_positions(requests.reshape(-1), trace_rows.shape[0], shot, space)
    rows = everything[positions].reshape(cells_x, levels, cells_y)

    far = parted(inner, "shot", 1)
    merged = swap(jnp.where(from_inner, inner, outer), "shot")
    scalars = jnp.stack([anchor - (shot - reach) * width, shot % 2])
    fields, own, far, inner, outer, beside, merged = finish(
        scalars,
        (velocity_sq, epsilon, delta),
        (far, inner, outer, beside, merged),
        across,
        along,
        base,
        rows,
    )

    far = parted(far, "shot", 1)
    merged = swap(merged, "shot")
    beside = swap(beside, "shot")
    nothing = jnp.zeros((), jnp.float32)
    outer = parted(outer + jnp.where(from_inner, nothing, merged), "shot", 2)
    inner = parted(inner + jnp.where(from_inner, merged, nothing) + far, "shot", -2)
    return (fields, own + beside + outer + inner)


def solution(mesh):
    in_specs = (
        P("shot", None, None, "space", None, None),
        P("space", "shot", None),
        P("space", "shot", None),
        P("space", "shot", None),
        P(("shot", "space"), None),
        P(),
        P(),
    )
    out_specs = (P("shot", None, "space", None, None), P("space", "shot", None))
    return jax.shard_map(local, mesh=mesh, in_specs=in_specs, out_specs=out_specs, check_vma=False)
```
